32 devices in a mesh: groups: 2 (over y), seq: 4 (over z), head: 2 (over x), tile: 2 (over core).
Axes of the slice: x: 2, y: 2, z: 4, core: 2. Of those that a mesh axis runs over, the one named last changes fastest.
Arguments:
- query_states: bfloat16 [4608, 3072], P(('groups', 'seq', 'tile'), 'head'), parts along dimension 0, may hold values from -5 to 5
- key_states: bfloat16 [4608, 3072], P(('groups', 'seq', 'tile'), 'head'), parts along dimension 0, may hold values from -5 to 5
- value_states: bfloat16 [4608, 3072], P(('groups', 'seq', 'tile'), 'head'), parts along dimension 0, may hold values from -6 to 6
- residual: bfloat16 [4608, 3072], P(('groups', 'seq', 'tile'), 'head'), parts along dimension 0, may hold values from -6 to 6
- out_weight: bfloat16 [3072, 3072], P(None, 'head'), may hold values from -0.109375 to 0.109375
- gate_scale: float32 [6144], P(('groups', 'head')), parts along dimension 0, may hold values from 2 to 8
Outputs:
- block_out: bfloat16 [4608, 3072], P(('groups', 'seq', 'tile'), 'head'), parts along dimension 0
The draws below stay inside these ranges and needn't reach their ends.
There are 2 independent parts, one for each index of `groups`. The reference program is written for one: setup_inputs(seed, part) draws one part's arguments, and reference() takes and returns one part's arrays. A program takes and returns all parts, laid end to end along the dimension named above; an argument that names none is the same for every part. Nothing has to cross between parts.
All inputs are finite; a program needn't handle non-finite values.
Results may differ from the reference program's by a relative error of at most 0.0065.
Values may be sent and summed in bfloat16 or wider, within the bound.
A program may use at most 128 MiB of HBM per device.

```python
import math
import jax
import jax.numpy as jnp
from jax import lax

D = 3072
HEADS = 24
HD = 128
SEQ = 2304


def draw_query_states(key, part):
    values_out = 1.4 * jax.random.truncated_normal(jax.random.fold_in(key, 1), -5.0 / 1.4, 5.0 / 1.4, (SEQ, D), jnp.float32)
    return values_out.astype(jnp.bfloat16)


def draw_key_states(key, part):
    values_out = 1.4 * jax.random.truncated_normal(jax.random.fold_in(key, 2), -5.0 / 1.4, 5.0 / 1.4, (SEQ, D), jnp.float32)
    return values_out.astype(jnp.bfloat16)


def shard_levels(rng, dims, split, low, high):
    factor_of = 1.0
    for axis_at, shards_of in split:
        steps = jax.random.uniform(jax.random.fold_in(jax.random.fold_in(rng, 6), axis_at), (shards_of,), jnp.float32, low / len(split), high / len(split))
        factor_of = factor_of * jnp.repeat(jnp.exp(steps), dims[axis_at] // shards_of).reshape((-1,) + (1,) * (len(dims) - 1 - axis_at))
    return factor_of


def scatter_about(stream_key, extent, spread, bound, split=(), held_as=jnp.bfloat16):
    result = spread * jax.random.normal(stream_key, extent, jnp.float32)
    if split:
        result = result * shard_levels(stream_key, extent, split, -0.22, 0.18)
    return jnp.clip(result, -bound, bound).astype(held_as)


def setup_inputs(seed: int = 0, part: int = 0) -> dict:
    splits = jax.random.split(jax.random.key(seed), 7)
    own_keys = jax.random.split(jax.random.fold_in(splits[6], part), 7)
    return {
        "query_states": draw_query_states(jax.random.fold_in(jax.random.fold_in(splits[6], part), 71), part),
        "key_states": draw_key_states(jax.random.fold_in(jax.random.fold_in(splits[6], part), 71), part),
        "value_states": scatter_about(own_keys[2], (SEQ, D), 1.0, 6.0, ((0, 8), (1, 2))),
        "residual": scatter_about(own_keys[3], (SEQ, D), 1.0, 6.0, ((0, 8), (1, 2))),
        "out_weight": scatter_about(splits[4], (D, D), D ** -0.5, 0.109375, ((1, 2),)),
        "gate_scale": jnp.clip(jnp.exp(math.log(8.0) - 1.3862944 * jax.random.uniform(own_keys[5], (D,), jnp.float32) ** shard_levels(own_keys[5], (D,), ((0, 2),), -0.2, 0.2)), 2.0, 8.0),
    }


def reference(query_states, key_states, value_states, residual, out_weight, gate_scale):
    score_scale = 1.0 / math.sqrt(HD)
    block_rows = math.gcd(SEQ, 1024)

    def one_head(head_index):
        query_head = lax.dynamic_slice_in_dim(query_states, head_index * HD, HD, 1)
        key_head = lax.dynamic_slice_in_dim(key_states, head_index * HD, HD, 1).astype(jnp.float32)
        value_head = lax.dynamic_slice_in_dim(value_states, head_index * HD, HD, 1)
        value_wide = value_head.astype(jnp.float32)

        def one_block(query_block):
            scores = jnp.dot(query_block.astype(jnp.float32), key_head.T, preferred_element_type=jnp.float32) * score_scale
            row_max = lax.optimization_barrier(jnp.max(scores, axis=1, keepdims=True))
            weights = jnp.exp(scores - row_max)
            denominator = lax.optimization_barrier(jnp.sum(weights, axis=1, keepdims=True))
            probs = weights.astype(jnp.bfloat16).astype(jnp.float32)
            summed = jnp.dot(probs, value_wide, preferred_element_type=jnp.float32)
            return (summed / denominator).astype(jnp.bfloat16)
        blocks = query_head.reshape(SEQ // block_rows, block_rows, HD)
        return lax.map(one_block, blocks).reshape(SEQ, HD)
    per_head = lax.map(one_head, jnp.arange(HEADS, dtype=jnp.int32))
    attended = jnp.transpose(per_head, (1, 0, 2)).reshape(SEQ, D)
    projected = jnp.dot(attended, out_weight, preferred_element_type=jnp.float32)
    return (residual.astype(jnp.float32) + gate_scale[None, :] * projected).astype(jnp.bfloat16)
```

```python
import functools
import math

import jax
import jax.numpy as jnp
from jax import lax
from jax.experimental import pallas as pl
from jax.experimental.pallas import tpu as pltpu
from jax.sharding import PartitionSpec as P

HD = 128
MESH = pl.DeviceIdType.MESH


def gathered(query_states, key_states, value_states, residual, out_weight, gate_scale):
    row_count = query_states.shape[0]
    heads_here = query_states.shape[1] // HD
    score_scale = 1.0 / math.sqrt(HD)
    query_heads = query_states.reshape(row_count, heads_here, HD)
    key_heads = lax.all_gather(key_states, ("seq", "tile"), axis=0, tiled=True).reshape(
        -1, heads_here, HD
    )
    value_heads = lax.all_gather(value_states, ("seq", "tile"), axis=0, tiled=True).reshape(
        -1, heads_here, HD
    )
    scores = (
        jnp.einsum("qhd,khd->hqk", query_heads, key_heads, preferred_element_type=jnp.float32)
        * score_scale
    )
    row_max = jnp.max(scores, axis=2)
    weights = jnp.exp(scores - row_max[:, :, None])
    denominator = jnp.sum(weights, axis=2)
    numerator = jnp.einsum(
        "hqk,khd->qhd",
        weights.astype(jnp.bfloat16),
        value_heads,
        preferred_element_type=jnp.float32,
    )
    attended = (
        (numerator / denominator.T[:, :, None])
        .astype(jnp.bfloat16)
        .reshape(row_count, heads_here * HD)
    )
    projected = jnp.dot(
        lax.all_gather(attended, "head", axis=1, tiled=True),
        out_weight,
        preferred_element_type=jnp.float32,
    )
    return (residual.astype(jnp.float32) + gate_scale[None, :] * projected).astype(jnp.bfloat16)


WINDOW = 2
LAST = 3


def kernel(
    nx,
    q_hbm,
    k_hbm,
    v_hbm,
    w_hbm,
    acc_out,
    rows_out,
    w_out,
    own,
    big,
    rel,
    o_out,
    att,
    w_buf,
    acc,
    out_sem,
    load_sem,
    big_sem,
    w_sem,
    in_send,
    in_recv,
    mid_send,
    mid_recv,
    o_send,
    o_recv,
    x_send,
    x_recv,
):
    z = lax.axis_index("seq")
    x = lax.axis_index("head")
    c = lax.axis_index("tile")
    rows = q_hbm.shape[0]
    columns = w_hbm.shape[1]
    pairs = own.shape[0]
    heads_here = 2 * pairs
    half = z // 2
    inner_z, outer_z = 1 + half, 3 * half
    inner = z == inner_z
    outer = z == outer_z
    send_order = [2, 3, 0, 1, 4, 5]
    take_order = [0, 1, 4, 2, 5, 3]

    def x_ahead(f):
        return lax.rem(x + f, nx)

    def x_behind(f):
        return lax.rem(x - f + nx, nx)

    def head_of(j, t):
        if j < 2:
            return 4 * half + 2 * j + t
        if j < 4:
            return 4 * (1 - half) + 2 * (j - 2) + t
        return 2 * j + t

    def place(j):
        return j + 2 if j < 4 else j - 4

    def block(b):
        return pl.ds(pl.multiple_of(b * rows, rows), rows)

    def columns_of(j, t):
        return pl.ds(pl.multiple_of(head_of(j, t) * HD, HD), HD)

    def load(j, t, a):
        return pltpu.make_async_copy(
            (q_hbm, k_hbm, v_hbm)[a].at[:, columns_of(j, t)], own.at[j, t, a], load_sem.at[j, t, a]
        )

    def big_load(j, a):
        return pltpu.make_async_copy(
            (q_hbm, k_hbm, v_hbm)[a].at[:, columns_of(j, c)],
            big.at[place(j), a, block(3)],
            big_sem.at[place(j), a],
        )

    for j in send_order:
        for t in range(2):
            for a in range(3):
                load(j, t, a).start()

    barrier = pltpu.get_barrier_semaphore()
    pl.semaphore_signal(barrier, inc=1, device_id={"tile": 1 - c}, device_id_type=MESH)
    for f in range(1, nx):
        pl.semaphore_signal(barrier, inc=1, device_id={"head": x_ahead(f)}, device_id_type=MESH)

    @pl.when(inner)
    def _():
        pl.semaphore_signal(barrier, inc=1, device_id={"seq": 3 - z}, device_id_type=MESH)
        pl.semaphore_wait(barrier, nx + 1)
        for t in range(2):
            pl.semaphore_signal(
                barrier, inc=1, device_id={"seq": outer_z, "tile": t}, device_id_type=MESH
            )

    @pl.when(outer)
    def _():
        pl.semaphore_wait(barrier, nx + 2)

    def arrays(j, b):
        return [(0, 3)] if j < 4 or b == 2 else [(1, 3), (0, 1)]

    def in_copy(j, t, b, device, span):
        low, high = span
        dst = rel.at[j - 2, :, block(b)] if j in (2, 3) else big.at[place(j), low:high, block(b)]
        part = 0 if high == 3 else 1
        return pltpu.make_async_remote_copy(
            src_ref=own.at[j, t, low:high],
            dst_ref=dst,
            send_sem=in_send.at[j, t, part],
            recv_sem=in_recv.at[place(j), b, part],
            device_id=device,
            device_id_type=MESH,
        )

    def edge_copy(j, t, span):
        return in_copy(j, t, (c + t) % 2, {"seq": inner_z, "tile": t}, span)

    def sibling_copy(j):
        return in_copy(j, 1 - c, 2, {"tile": 1 - c}, (0, 3))

    def arrived(j, b, span):
        in_copy(j, c, b, {"tile": 1 - c}, span).wait_recv()

    def mid_copy(j, b):
        if j < 4:
            at, low = j, 0
            src = own.at[j, c] if b == 3 else rel.at[j - 2, :, block(b)]
        else:
            at, low = place(j), 1
            src = own.at[j, c, 1:3] if b == 3 else big.at[at, 1:3, block(b)]
        return pltpu.make_async_remote_copy(
            src_ref=src,
            dst_ref=big.at[at, low:3, block(4 + b)],
            send_sem=mid_send.at[at, b],
            recv_sem=mid_recv.at[at, b],
            device_id={"seq": 3 - z},
            device_id_type=MESH,
        )

    def feature(j, t, f):
        if j == LAST:
            return rows_out.at[:, pl.ds(pl.multiple_of((t * nx + f) * HD, HD), HD)]
        return att.at[j, t, f]

    def o_copy(j, b, far=0):
        there = half + far * (1 - 2 * half)
        is_inner = b // 2
        flip = ((b + 1) // 2) % 2
        return pltpu.make_async_remote_copy(
            src_ref=o_out.at[place(j), 4 * far + b],
            dst_ref=feature(j + 2 * far, c, 0),
            send_sem=o_send.at[place(j), 4 * far + b],
            recv_sem=o_recv.at[j + 2 * far, c],
            device_id={
                "seq": is_inner * (1 + there) + (1 - is_inner) * 3 * there,
                "tile": (c + flip) % 2,
            },
            device_id_type=MESH,
        )

    def o_arrival(j, t):
        return pltpu.make_async_remote_copy(
            src_ref=o_out.at[0, 0],
            dst_ref=feature(j, t, 0),
            send_sem=o_send.at[0, 0],
            recv_sem=o_recv.at[j, t],
            device_id={"tile": 1 - c},
            device_id_type=MESH,
        )

    def x_copy(j, t, f):
        return pltpu.make_async_remote_copy(
            src_ref=feature(j, t, 0),
            dst_ref=feature(j, t, f),
            send_sem=x_send.at[j, t, f],
            recv_sem=x_recv.at[j, t, f],
            device_id={"head": x_ahead(f)},
            device_id_type=MESH,
        )

    queue = [(j, b, 0) for j in (2, 3) for b in (3, 2)]
    queue += [(j, b, 0) for j in (2, 3) for b in (0, 1)]
    queue += [(j, b, 0) for j in (4, 5) for b in (3, 2)]
    queue += [(j, b, 0) for j in (4, 5) for b in (0, 1)]
    queue += [(j, b, 1) for bs in ((0, 1), (3, 2)) for j in (0, 1) for b in bs]

    def queued(n):
        j, b, far = queue[n]
        return o_copy(j, b, 1) if far else mid_copy(j, b)

    def pump(first, end=None):
        for n in range(first, first + 1 if end is None else end):
            j, b, far = queue[n]
            if not far:
                if b == 3:
                    for a in range(3):
                        load(j, c, a).wait()
                else:
                    arrived(j, b, arrays(j, b)[0])
            if n >= WINDOW:
                queued(n - WINDOW).wait_send()
            queued(n).start()

    def pumps(*steps):
        return [(at, functools.partial(pump, n)) for at, n in steps]

    def send_sibling(j):
        for a in range(3):
            load(j, 1 - c, a).wait()
        sibling_copy(j).start()

    @pl.when(outer)
    def _():
        edges = [(j, t, (0, 3)) for j in (2, 3, 0, 1) for t in range(2)]
        edges += [(j, t, (1, 3)) for j in (4, 5) for t in range(2)]
        edges += [(j, t, (0, 1)) for j in (4, 5) for t in range(2)]
        for n, (j, t, (low, high)) in enumerate(edges):
            for a in range(low, high):
                load(j, t, a).wait()
            if n >= WINDOW:
                edge_copy(*edges[n - WINDOW]).wait_send()
            edge_copy(j, t, (low, high)).start()
        for edge in edges[-WINDOW:]:
            edge_copy(*edge).wait_send()

    @pl.when(inner)
    def _():
        pump(0)
        send_sibling(2)
        send_sibling(3)
        pump(1)
        for j in (0, 1, 4, 5):
            send_sibling(j)
        for j in (0, 1):
            for a in range(3):
                load(j, c, a).wait()
        for j in (0, 1, 4, 5):
            for a in range(3):
                big_load(j, a).start()

    w_loads = {}
    for j in take_order:
        for t in range(2):
            for f in range(nx):
                head = x_behind(f) * heads_here + head_of(j, t)
                copy = pltpu.make_async_copy(
                    w_hbm.at[pl.ds(pl.multiple_of(head * HD, HD), HD)],
                    (w_out if j == LAST else w_buf.at[j]).at[pl.ds((t * nx + f) * HD, HD)],
                    w_sem.at[j, t * nx + f],
                )
                copy.start()
                w_loads[j, t, f] = copy

    factor = math.log2(math.e) / math.sqrt(HD)
    keys = 8 * rows
    parts = 3

    def attend(at, b):
        queries = big[at, 0, block(b)]
        step = keys // parts
        for p in range(parts):
            span = pl.ds(p * step, step)
            scores = lax.dot_general(
                queries,
                big[at, 1, span],
                (((1,), (1,)), ((), ())),
                preferred_element_type=jnp.float32,
            )
            part_max = jnp.max(scores, axis=1, keepdims=True)
            new_max = jnp.maximum(row_max, part_max) if p else part_max
            weights = jnp.exp2((scores - new_max) * factor)
            part_sum = jnp.sum(weights, axis=1, keepdims=True)
            product = jnp.dot(
                weights.astype(jnp.bfloat16), big[at, 2, span], preferred_element_type=jnp.float32
            )
            if p:
                scale = jnp.exp2((row_max - new_max) * factor)
                denominator = denominator * scale + part_sum
                numerator = numerator * scale + product
            else:
                denominator, numerator = part_sum, product
            row_max = new_max
        return (numerator / denominator).astype(jnp.bfloat16)

    def ready(j):
        for a in range(3):
            big_load(j, a).wait()
        for b in range(3):
            for span in arrays(j, b):
                if j < 4 or span == (0, 1):
                    arrived(j, b, span)
        for b in range(4):
            mid_copy(j + 2 if j < 2 else j, b).wait_recv()

    def compute(j, between):
        at = place(j)
        count = 8 if j < 2 else 4

        def step(i, carry):
            b = (i + 4) % 8 if j < 2 else i
            o_out[at, b] = attend(at, b)

            @pl.when(b < 3)
            def _():
                o_copy(j, b).start()

            for when, todo in between:
                pl.when(i == when)(todo)

            return carry

        lax.fori_loop(0, count, step, 0)
        att[j, c, 0] = o_out[at, 3]
        for f in range(1, nx):
            x_copy(j, c, f).start()

    def take(j, t):
        o_arrival(j, t).wait_recv()
        for f in range(1, nx):
            x_copy(j, t, f).start()

    def take_outer(j):
        @pl.when(outer)
        def _():
            take(j, c)
            take(j, 1 - c)

    width = math.gcd(columns, 512)

    def out_copy(start):
        cols = pl.ds(start, width)
        return pltpu.make_async_copy(
            acc.at[:, cols], acc_out.at[:, cols], out_sem.at[start // width]
        )

    def project(j, first=False, last=False):
        for t in range(2):
            for f in range(nx):
                w_loads[j, t, f].wait()
                if f:
                    x_copy(j, t, f).wait_recv()
        rows_in = jnp.concatenate([att[j, t, f] for t in range(2) for f in range(nx)], axis=1)
        for start in range(0, columns, width):
            cols = slice(start, start + width)
            part = jnp.dot(rows_in, w_buf[j, :, cols], preferred_element_type=jnp.float32)
            total = part if first else acc[:, cols] + part
            acc[:, cols] = total
            if last:
                out_copy(start).start()

    @pl.when(inner)
    def _():
        pump(2, 8)
        ready(0)
        compute(0, pumps((3, 8), (6, 9)))
        ready(1)
        compute(1, pumps((0, 10), (3, 11), (5, 12)))
        take(0, 1 - c)
        pump(13)
        take(1, 1 - c)

    take_outer(0)
    take_outer(1)
    project(0, first=True)

    @pl.when(inner)
    def _():
        pump(14, 16)

    project(1)

    @pl.when(inner)
    def _():
        ready(4)
        compute(4, pumps((1, 16), (3, 17)))
        ready(5)
        taken = [(1, functools.partial(take, 4, 1 - c))]
        compute(5, pumps((0, 18), (1, 19), (2, 20), (3, 21)) + taken)
        pump(22)
        take(5, 1 - c)
        take(2, c)
        pump(23)

    take_outer(4)
    take_outer(2)
    take_outer(3)
    project(4)
    take_outer(5)

    @pl.when(inner)
    def _():
        take(2, 1 - c)
        take(3, c)

    project(5)

    @pl.when(inner)
    def _():
        take(3, 1 - c)

    project(2, last=True)
    for start in range(0, columns, width):
        out_copy(start).wait()
    for t in range(2):
        for f in range(nx):
            w_loads[LAST, t, f].wait()
            if f:
                x_copy(LAST, t, f).wait_recv()

    @pl.when(inner)
    def _():
        for j in range(pairs):
            sibling_copy(j).wait_send()
            if j not in (2, 3):
                for b in range(3):
                    o_copy(j, b).wait_send()
        for n in range(len(queue) - WINDOW, len(queue)):
            queued(n).wait_send()

    for j in range(pairs):
        for t in range(2):
            for f in range(1, nx):
                x_copy(j, t, f).wait_send()


def exchanged(nx, query_states, key_states, value_states, out_weight, residual, gate_scale):
    rows, width = query_states.shape
    columns = out_weight.shape[1]
    pairs = width // HD // 2
    jobs = pairs - 2
    bf16 = jnp.bfloat16
    dma = pltpu.SemaphoreType.DMA
    anywhere = pl.BlockSpec(memory_space=pltpu.HBM)
    acc, rows_in, last_weight = pl.pallas_call(
        functools.partial(kernel, nx),
        out_shape=[
            jax.ShapeDtypeStruct((rows, columns), jnp.float32),
            jax.ShapeDtypeStruct((rows, 2 * nx * HD), bf16),
            jax.ShapeDtypeStruct((2 * nx * HD, columns), bf16),
        ],
        in_specs=[anywhere] * 4,
        out_specs=[pl.BlockSpec(memory_space=pl.ANY)] * 3,
        scratch_shapes=[
            pltpu.VMEM((pairs, 2, 3, rows, HD), bf16),
            pltpu.VMEM((jobs, 3, 8 * rows, HD), bf16),
            pltpu.VMEM((2, 3, 3 * rows, HD), bf16),
            pltpu.VMEM((jobs, 8, rows, HD), bf16),
            pltpu.VMEM((pairs, 2, nx, rows, HD), bf16),
            pltpu.VMEM((pairs, 2 * nx * HD, columns), bf16),
            pltpu.VMEM((rows, columns), jnp.float32),
            dma((columns // math.gcd(columns, 512),)),
            dma((pairs, 2, 3)),
            dma((jobs, 3)),
            dma((pairs, 2 * nx)),
            dma((pairs, 2, 2)),
            dma((pairs, 3, 2)),
            dma((jobs, 4)),
            dma((jobs, 4)),
            dma((jobs, 8)),
            dma((pairs, 2)),
            dma((pairs, 2, nx)),
            dma((pairs, 2, nx)),
        ],
        compiler_params=pltpu.CompilerParams(
            collective_id=0, has_side_effects=True, vmem_limit_bytes=44 << 20
        ),
    )(
        *(
            pltpu.with_memory_space_constraint(array, pltpu.HBM)
            for array in (query_states, key_states, value_states, out_weight)
        )
    )
    projected = acc + jnp.dot(rows_in, last_weight, preferred_element_type=jnp.float32)
    return (residual.astype(jnp.float32) + gate_scale[None, :] * projected).astype(bf16)


def solution(mesh):
    n, nx = mesh.shape["seq"], mesh.shape["head"]

    def per_device(query_states, key_states, value_states, residual, out_weight, gate_scale):
        heads_here = query_states.shape[1] // HD
        if n != 4 or mesh.shape["tile"] != 2 or heads_here != 12:
            return gathered(
                query_states, key_states, value_states, residual, out_weight, gate_scale
            )
        return exchanged(
            nx, query_states, key_states, value_states, out_weight, residual, gate_scale
        )

    placed = (
        P(("groups", "seq", "tile"), "head"),
        P(("groups", "seq", "tile"), "head"),
        P(("groups", "seq", "tile"), "head"),
        P(("groups", "seq", "tile"), "head"),
        P(None, "head"),
        P(("groups", "head")),
    )
    return jax.shard_map(
        per_device,
        mesh=mesh,
        in_specs=placed,
        out_specs=P(("groups", "seq", "tile"), "head"),
        check_vma=False,
    )
```

```python
import functools
import math

import jax
import jax.numpy as jnp
from jax import lax
from jax.experimental import pallas as pl
from jax.experimental.pallas import tpu as pltpu
from jax.sharding import PartitionSpec as P

HD = 128
MESH = pl.DeviceIdType.MESH


def gathered(query_states, key_states, value_states, residual, out_weight, gate_scale):
    row_count = query_states.shape[0]
    heads_here = query_states.shape[1] // HD
    score_scale = 1.0 / math.sqrt(HD)
    query_heads = query_states.reshape(row_count, heads_here, HD)
    key_heads = lax.all_gather(key_states, ("seq", "tile"), axis=0, tiled=True).reshape(
        -1, heads_here, HD
    )
    value_heads = lax.all_gather(value_states, ("seq", "tile"), axis=0, tiled=True).reshape(
        -1, heads_here, HD
    )
    scores = (
        jnp.einsum("qhd,khd->hqk", query_heads, key_heads, preferred_element_type=jnp.float32)
        * score_scale
    )
    row_max = jnp.max(scores, axis=2)
    weights = jnp.exp(scores - row_max[:, :, None])
    denominator = jnp.sum(weights, axis=2)
    numerator = jnp.einsum(
        "hqk,khd->qhd",
        weights.astype(jnp.bfloat16),
        value_heads,
        preferred_element_type=jnp.float32,
    )
    attended = (
        (numerator / denominator.T[:, :, None])
        .astype(jnp.bfloat16)
        .reshape(row_count, heads_here * HD)
    )
    projected = jnp.dot(
        lax.all_gather(attended, "head", axis=1, tiled=True),
        out_weight,
        preferred_element_type=jnp.float32,
    )
    return (residual.astype(jnp.float32) + gate_scale[None, :] * projected).astype(jnp.bfloat16)


WINDOW = 3
LAST = (5, 3)
PART = 256


def kernel(
    nx,
    q_hbm,
    k_hbm,
    v_hbm,
    w_hbm,
    acc_out,
    rows_out,
    w_out,
    own,
    big,
    rel,
    o_out,
    att,
    w_buf,
    acc,
    max_buf,
    sum_buf,
    num_buf,
    out_sem,
    own_sem,
    load_sem,
    big_sem,
    w_sem,
    edge_send,
    sib_send,
    in_recv,
    home_recv,
    q_recv,
    mid_send,
    mid_recv,
    o_send,
    o_recv,
    x_send,
    x_recv,
):
    z = lax.axis_index("seq")
    x = lax.axis_index("head")
    c = lax.axis_index("tile")
    rows = q_hbm.shape[0]
    columns = w_hbm.shape[1]
    pairs = own.shape[0]
    heads_here = 2 * pairs
    half = z // 2
    inner_z, outer_z = 1 + half, 3 * half
    inner = z == inner_z
    outer = z == outer_z
    send_order = [2, 3, 0, 1, 4, 5]
    take_order = [0, 1, 4, 2, 5, 3]

    def x_ahead(f):
        return lax.rem(x + f, nx)

    def x_behind(f):
        return lax.rem(x - f + nx, nx)

    def head_of(j, t):
        if j < 2:
            return 4 * half + 2 * j + t
        if j < 4:
            return 4 * (1 - half) + 2 * (j - 2) + t
        return 2 * j + t

    def place(j):
        return j + 2 if j < 4 else j - 4

    def block(b):
        return pl.ds(pl.multiple_of(b * rows, rows), rows)

    def columns_of(j, t):
        return pl.ds(pl.multiple_of(head_of(j, t) * HD, HD), HD)

    arguments = (q_hbm, k_hbm, v_hbm)

    def load(j, t):
        for a in range(3):
            pltpu.make_async_copy(
                arguments[a].at[:, columns_of(j, t)], own.at[j, t, a], load_sem.at[j, t]
            ).start()

    def loaded(j, t):
        pltpu.make_async_copy(own.at[j, t], own.at[j, t], load_sem.at[j, t]).wait()

    def big_load(j):
        for a in range(3):
            pltpu.make_async_copy(
                arguments[a].at[:, columns_of(j, c)],
                big.at[place(j), a, block(3)],
                big_sem.at[place(j)],
            ).start()

    for j in send_order:
        for t in range(2):
            load(j, t)

    barrier = pltpu.get_barrier_semaphore()
    pl.semaphore_signal(barrier, inc=1, device_id={"tile": 1 - c}, device_id_type=MESH)
    for f in range(1, nx):
        pl.semaphore_signal(barrier, inc=1, device_id={"head": x_ahead(f)}, device_id_type=MESH)

    @pl.when(inner)
    def _():
        pl.semaphore_signal(barrier, inc=1, device_id={"seq": 3 - z}, device_id_type=MESH)
        pl.semaphore_wait(barrier, nx + 1)
        for t in range(2):
            pl.semaphore_signal(
                barrier, inc=1, device_id={"seq": outer_z, "tile": t}, device_id_type=MESH
            )

    @pl.when(outer)
    def _():
        pl.semaphore_wait(barrier, nx + 2)

    def in_copy(j, t, b, device, span, send_sem):
        low, high = span
        at = place(j)
        if j < 2:
            recv_sem = home_recv.at[j]
        elif high == 1:
            recv_sem = q_recv.at[at]
        else:
            recv_sem = in_recv.at[j - 2, b]
        dst = rel.at[j - 2, :, block(b)] if j in (2, 3) else big.at[at, low:high, block(b)]
        return pltpu.make_async_remote_copy(
            src_ref=own.at[j, t, low:high],
            dst_ref=dst,
            send_sem=send_sem,
            recv_sem=recv_sem,
            device_id=device,
            device_id_type=MESH,
        )

    def sibling_copy(j):
        return in_copy(j, 1 - c, 2, {"tile": 1 - c}, (0, 3), sib_send)

    def landed(ref, send_sem, recv_sem):
        return pltpu.make_async_remote_copy(
            src_ref=ref,
            dst_ref=ref,
            send_sem=send_sem,
            recv_sem=recv_sem,
            device_id={"tile": 1 - c},
            device_id_type=MESH,
        )

    def mid_copy(j, b, send_sem):
        if j < 4:
            at, low = j, 0
            src = own.at[j, c] if b == 3 else rel.at[j - 2, :, block(b)]
        else:
            at, low = place(j), 1
            src = own.at[j, c, 1:3] if b == 3 else big.at[at, 1:3, block(b)]
        return pltpu.make_async_remote_copy(
            src_ref=src,
            dst_ref=big.at[at, low:3, block(4 + b)],
            send_sem=send_sem,
            recv_sem=mid_recv.at[at],
            device_id={"seq": 3 - z},
            device_id_type=MESH,
        )

    def feature(j, t, f):
        if j in LAST:
            start = (2 * nx * LAST.index(j) + 2 * f + t) * HD
            return rows_out.at[:, pl.ds(pl.multiple_of(start, HD), HD)]
        return att.at[j, f, t]

    def peers(j):
        if j in LAST:
            start = 2 * nx * LAST.index(j) * HD
            return rows_out.at[:, start + 2 * HD : start + 2 * nx * HD]
        return att.at[j, 1:nx]

    def weights_of(j):
        if j in LAST:
            start = 2 * nx * LAST.index(j) * HD
            return w_out.at[start : start + 2 * nx * HD]
        return w_buf.at[j]

    def o_copy(j, b, far=0, send_sem=None):
        there = half + far * (1 - 2 * half)
        is_inner = b // 2
        flip = ((b + 1) // 2) % 2
        return pltpu.make_async_remote_copy(
            src_ref=o_out.at[place(j), 4 * far + b],
            dst_ref=feature(j + 2 * far, c, 0),
            send_sem=o_send.at[place(j)] if send_sem is None else send_sem,
            recv_sem=o_recv.at[j + 2 * far, c],
            device_id={
                "seq": is_inner * (1 + there) + (1 - is_inner) * 3 * there,
                "tile": (c + flip) % 2,
            },
            device_id_type=MESH,
        )

    def o_arrival(j, t):
        return pltpu.make_async_remote_copy(
            src_ref=o_out.at[0, 0],
            dst_ref=feature(j, t, 0),
            send_sem=o_send.at[0],
            recv_sem=o_recv.at[j, t],
            device_id={"tile": 1 - c},
            device_id_type=MESH,
        )

    def own_copy(j):
        return pltpu.make_async_copy(o_out.at[place(j), 3], feature(j, c, 0), own_sem)

    def x_copy(j, t, f, src=None):
        return pltpu.make_async_remote_copy(
            src_ref=feature(j, t, 0) if src is None else src,
            dst_ref=feature(j, t, f),
            send_sem=x_send.at[j],
            recv_sem=x_recv.at[j],
            device_id={"head": x_ahead(f)},
            device_id_type=MESH,
        )

    queue = [(j, b, 0) for j in (2, 3) for b in (3, 2)]
    queue += [(j, b, 0) for j in (2, 3) for b in (0, 1)]
    queue += [(j, b, 0) for j in (4, 5) for b in (3, 2)]
    queue += [(j, b, 0) for j in (4, 5) for b in (0, 1)]
    queue += [(0, 0, 1), (0, 3, 1), (0, 1, 1), (1, 0, 1)]
    queue += [(0, 2, 1), (1, 1, 1), (1, 3, 1), (1, 2, 1)]

    def queued(n):
        j, b, far = queue[n]
        send_sem = mid_send.at[n % WINDOW]
        return o_copy(j, b, 1, send_sem) if far else mid_copy(j, b, send_sem)

    def pump(first, end=None):
        for n in range(first, first + 1 if end is None else end):
            j, b, far = queue[n]
            if not far:
                if b == 3:
                    loaded(j, c)
                else:
                    span = (1, 3) if j > 3 and b < 2 else (0, 3)
                    in_copy(j, c, b, {"tile": 1 - c}, span, sib_send).wait_recv()
            if n >= WINDOW:
                queued(n - WINDOW).wait_send()
            queued(n).start()

    def pumps(*steps):
        return [(at, functools.partial(pump, n)) for at, n in steps]

    def send_sibling(j):
        loaded(j, 1 - c)
        sibling_copy(j).start()

    @pl.when(inner)
    def _():
        pump(0)
        send_sibling(2)
        send_sibling(3)
        pump(1)
        for j in (0, 1, 4, 5):
            send_sibling(j)
        for j in (0, 1):
            loaded(j, c)
        for j in (0, 1, 4, 5):
            big_load(j)

    for j in take_order:
        weights = weights_of(j)
        for t in range(2):
            for f in range(nx):
                head = x_behind(f) * heads_here + head_of(j, t)
                pltpu.make_async_copy(
                    w_hbm.at[pl.ds(pl.multiple_of(head * HD, HD), HD)],
                    weights.at[pl.ds((2 * f + t) * HD, HD)],
                    w_sem.at[j],
                ).start()

    def weights_loaded(j):
        weights = weights_of(j)
        pltpu.make_async_copy(weights, weights, w_sem.at[j]).wait()

    factor = math.log2(math.e) / math.sqrt(HD)
    keys = 8 * rows
    early = 4 * rows // PART * PART

    def fold(at, b, low, high, state=None):
        queries = big[at, 0, block(b)]
        for start in range(low, high, PART):
            span = pl.ds(start, PART)
            scores = lax.dot_general(
                queries,
                big[at, 1, span],
                (((1,), (1,)), ((), ())),
                preferred_element_type=jnp.float32,
            )
            new_max = jnp.max(scores, axis=1, keepdims=True)
            if state is not None:
                row_max, denominator, numerator = state
                new_max = jnp.maximum(row_max, new_max)
            weights = jnp.exp2((scores - new_max) * factor)
            total = jnp.sum(weights, axis=1, keepdims=True)
            product = jnp.dot(
                weights.astype(jnp.bfloat16), big[at, 2, span], preferred_element_type=jnp.float32
            )
            if state is not None:
                scale = jnp.exp2((row_max - new_max) * factor)
                total = denominator * scale + total
                product = numerator * scale + product
            state = new_max, total, product
        return state

    def ready(j):
        at = place(j)
        pltpu.make_async_copy(own.at[j, c], own.at[j, c], big_sem.at[at]).wait()
        if j < 2:
            landed(big.at[at, :, : 3 * rows], sib_send, home_recv.at[j]).wait_recv()
        else:
            landed(big.at[at, 0, : 2 * rows], sib_send, q_recv.at[at]).wait_recv()

    def ready_far(j):
        at = place(j)
        low = 0 if j < 2 else 1
        landed(big.at[at, low:3, 4 * rows :], sib_send, mid_recv.at[at]).wait_recv()

    def begin(j):
        at = place(j)

        def step(b, carry):
            row_max, denominator, num_buf[at, b] = fold(at, b, 0, early)
            max_buf[at, b] = jnp.broadcast_to(row_max, (rows, HD))
            sum_buf[at, b] = jnp.broadcast_to(denominator, (rows, HD))
            return carry

        lax.fori_loop(0, 4, step, 0)

    def compute(j, between):
        at = place(j)
        count = 8 if j < 2 else 4

        def step(i, carry):
            if j < 2:
                b = (i + 4) % 8
                _, denominator, numerator = fold(at, b, 0, keys)
            else:
                b = i
                row_max, denominator, numerator = fold(at, b, early, keys)
                row_max = jnp.broadcast_to(row_max, (rows, HD))
                new_max = jnp.maximum(max_buf[at, b], row_max)
                before = jnp.exp2((max_buf[at, b] - new_max) * factor)
                after = jnp.exp2((row_max - new_max) * factor)
                denominator = sum_buf[at, b] * before + denominator * after
                numerator = num_buf[at, b] * before + numerator * after
            o_out[at, b] = (numerator / denominator).astype(jnp.bfloat16)

            @pl.when(b < 3)
            def _():
                o_copy(j, b).start()

            for when, todo in between:
                pl.when(i == when)(todo)

            return carry

        lax.fori_loop(0, count, step, 0)
        for f in range(1, nx):
            x_copy(j, c, f, o_out.at[at, 3]).start()
        if j in LAST:
            own_copy(j).start()
        else:
            att[j, 0, c] = o_out[at, 3]

    def take(j, t):
        o_arrival(j, t).wait_recv()
        for f in range(1, nx):
            x_copy(j, t, f).start()

    def take_outer(j):
        @pl.when(outer)
        def _():
            take(j, c)
            take(j, 1 - c)

    @pl.when(outer)
    def _():
        edges = [(j, t, (0, 3)) for j in (2, 3, 0, 1) for t in range(2)]
        edges += [(j, t, (1, 3)) for j in (4, 5) for t in range(2)]
        edges += [(j, t, (0, 1)) for j in (4, 5) for t in range(2)]

        def edge(n):
            j, t, span = edges[n]
            device = {"seq": inner_z, "tile": t}
            return in_copy(j, t, (c + t) % 2, device, span, edge_send.at[n % WINDOW])

        for n, (j, t, (_, high)) in enumerate(edges):
            if high == 3:
                loaded(j, t)
            if n >= WINDOW:
                edge(n - WINDOW).wait_send()
            edge(n).start()
            if n in (13, 15):
                take(n // 15, c)
                take(n // 15, 1 - c)
        for n in range(len(edges) - WINDOW, len(edges)):
            edge(n).wait_send()

    width = math.gcd(columns, 512)

    def project(j, first=False, last=False):
        weights_loaded(j)
        landed(peers(j), x_send.at[j], x_recv.at[j]).wait_recv()
        rows_in = jnp.concatenate([att[j, f, t] for f in range(nx) for t in range(2)], axis=1)
        for start in range(0, columns, width):
            cols = slice(start, start + width)
            part = jnp.dot(rows_in, w_buf[j, :, cols], preferred_element_type=jnp.float32)
            total = part if first else acc[:, cols] + part
            acc[:, cols] = total
            if last:
                pltpu.make_async_copy(acc.at[:, cols], acc_out.at[:, cols], out_sem).start()

    @pl.when(inner)
    def _():
        pump(2, 9)
        ready(0)
        ready_far(0)
        compute(0, pumps((3, 9), (6, 10)))
        ready(1)
        ready_far(1)
        compute(1, pumps((1, 11), (4, 12), (7, 13)) + [(0, functools.partial(take, 0, 1 - c))])
        take(1, 1 - c)
        pump(14)

    project(0, first=True)

    @pl.when(inner)
    def _():
        ready(4)
        begin(4)
        pump(15)

    project(1)

    @pl.when(inner)
    def _():
        ready_far(4)
        compute(4, pumps((2, 16)))
        ready(5)
        begin(5)
        pump(17)
        pump(18)
        ready_far(5)
        taken = [(0, functools.partial(take, 4, 1 - c)), (2, functools.partial(take, 2, c))]
        compute(5, pumps((1, 19), (3, 20)) + taken)
        take(5, 1 - c)
        pump(21)

    take_outer(4)
    take_outer(2)
    project(4)

    @pl.when(outer)
    def _():
        take(5, c)
        take(3, c)
        take(5, 1 - c)
        take(3, 1 - c)

    @pl.when(inner)
    def _():
        pump(22, 24)
        take(2, 1 - c)
        take(3, c)
        take(3, 1 - c)

    project(2, last=True)
    pltpu.make_async_copy(acc, acc_out, out_sem).wait()
    for j in LAST:
        weights_loaded(j)
    for j in LAST:
        landed(peers(j), x_send.at[j], x_recv.at[j]).wait_recv()

    @pl.when(inner)
    def _():
        own_copy(5).wait()

    @pl.when(inner)
    def _():
        landed(own.at[:, 0], sib_send, sib_send).wait_send()
        for at in range(o_out.shape[0]):
            landed(o_out.at[at, :3], o_send.at[at], sib_send).wait_send()
        for n in range(len(queue) - WINDOW, len(queue)):
            queued(n).wait_send()

    for j in range(pairs):
        landed(att.at[j, 1:nx], x_send.at[j], sib_send).wait_send()


def exchanged(nx, query_states, key_states, value_states, out_weight, residual, gate_scale):
    rows, width = query_states.shape
    columns = out_weight.shape[1]
    pairs = width // HD // 2
    jobs = pairs - 2
    bf16 = jnp.bfloat16
    dma = pltpu.SemaphoreType.DMA
    anywhere = pl.BlockSpec(memory_space=pltpu.HBM)
    acc, rows_in, last_weight = pl.pallas_call(
        functools.partial(kernel, nx),
        out_shape=[
            jax.ShapeDtypeStruct((rows, columns), jnp.float32),
            jax.ShapeDtypeStruct((rows, 2 * len(LAST) * nx * HD), bf16),
            jax.ShapeDtypeStruct((2 * len(LAST) * nx * HD, columns), bf16),
        ],
        in_specs=[anywhere] * 4,
        out_specs=[pl.BlockSpec(memory_space=pl.ANY)] * 3,
        scratch_shapes=[
            pltpu.VMEM((pairs, 2, 3, rows, HD), bf16),
            pltpu.VMEM((jobs, 3, 8 * rows, HD), bf16),
            pltpu.VMEM((2, 3, 3 * rows, HD), bf16),
            pltpu.VMEM((jobs, 8, rows, HD), bf16),
            pltpu.VMEM((pairs, nx, 2, rows, HD), bf16),
            pltpu.VMEM((pairs, 2 * nx * HD, columns), bf16),
            pltpu.VMEM((rows, columns), jnp.float32),
            pltpu.VMEM((2, 4, rows, HD), jnp.float32),
            pltpu.VMEM((2, 4, rows, HD), jnp.float32),
            pltpu.VMEM((2, 4, rows, HD), jnp.float32),
            dma,
            dma,
            dma((pairs, 2)),
            dma((jobs,)),
            dma((pairs,)),
            dma((WINDOW,)),
            dma,
            dma((pairs - 2, 3)),
            dma((2,)),
            dma((2,)),
            dma((WINDOW,)),
            dma((jobs,)),
            dma((jobs,)),
            dma((pairs, 2)),
            dma((pairs,)),
            dma((pairs,)),
        ],
        compiler_params=pltpu.CompilerParams(
            collective_id=0, has_side_effects=True, vmem_limit_bytes=44 << 20
        ),
    )(
        *(
            pltpu.with_memory_space_constraint(array, pltpu.HBM)
            for array in (query_states, key_states, value_states, out_weight)
        )
    )
    projected = acc + jnp.dot(rows_in, last_weight, preferred_element_type=jnp.float32)
    return (residual.astype(jnp.float32) + gate_scale[None, :] * projected).astype(bf16)


def solution(mesh):
    n, nx = mesh.shape["seq"], mesh.shape["head"]

    def per_device(query_states, key_states, value_states, residual, out_weight, gate_scale):
        heads_here = query_states.shape[1] // HD
        fits = query_states.shape[0] % 32 == 0 and 8 * query_states.shape[0] % PART == 0
        if n != 4 or nx < 2 or mesh.shape["tile"] != 2 or heads_here != 12 or not fits:
            return gathered(
                query_states, key_states, value_states, residual, out_weight, gate_scale
            )
        return exchanged(
            nx, query_states, key_states, value_states, out_weight, residual, gate_scale
        )

    placed = (
        P(("groups", "seq", "tile"), "head"),
        P(("groups", "seq", "tile"), "head"),
        P(("groups", "seq", "tile"), "head"),
        P(("groups", "seq", "tile"), "head"),
        P(None, "head"),
        P(("groups", "head")),
    )
    return jax.shard_map(
        per_device,
        mesh=mesh,
        in_specs=placed,
        out_specs=P(("groups", "seq", "tile"), "head"),
        check_vma=False,
    )
```

```python
import functools
import math

import jax
import jax.numpy as jnp
from jax import lax
from jax.experimental import pallas as pl
from jax.experimental.pallas import tpu as pltpu
from jax.sharding import PartitionSpec as P

HD = 128
MESH = pl.DeviceIdType.MESH


def gathered(query_states, key_states, value_states, residual, out_weight, gate_scale):
    row_count = query_states.shape[0]
    heads_here = query_states.shape[1] // HD
    score_scale = 1.0 / math.sqrt(HD)
    query_heads = query_states.reshape(row_count, heads_here, HD)
    key_heads = lax.all_gather(key_states, ("seq", "tile"), axis=0, tiled=True).reshape(
        -1, heads_here, HD
    )
    value_heads = lax.all_gather(value_states, ("seq", "tile"), axis=0, tiled=True).reshape(
        -1, heads_here, HD
    )
    scores = (
        jnp.einsum("qhd,khd->hqk", query_heads, key_heads, preferred_element_type=jnp.float32)
        * score_scale
    )
    row_max = jnp.max(scores, axis=2)
    weights = jnp.exp(scores - row_max[:, :, None])
    denominator = jnp.sum(weights, axis=2)
    numerator = jnp.einsum(
        "hqk,khd->qhd",
        weights.astype(jnp.bfloat16),
        value_heads,
        preferred_element_type=jnp.float32,
    )
    attended = (
        (numerator / denominator.T[:, :, None])
        .astype(jnp.bfloat16)
        .reshape(row_count, heads_here * HD)
    )
    projected = jnp.dot(
        lax.all_gather(attended, "head", axis=1, tiled=True),
        out_weight,
        preferred_element_type=jnp.float32,
    )
    return (residual.astype(jnp.float32) + gate_scale[None, :] * projected).astype(jnp.bfloat16)


WINDOW = 3
LAST = (5, 3)
PART = 256


def kernel(
    nx,
    q_hbm,
    k_hbm,
    v_hbm,
    w_hbm,
    acc_out,
    rows_out,
    w_out,
    own,
    big,
    rel,
    o_out,
    att,
    w_buf,
    acc,
    max_buf,
    sum_buf,
    num_buf,
    out_sem,
    own_sem,
    load_sem,
    big_sem,
    w_sem,
    edge_send,
    sib_send,
    in_recv,
    home_recv,
    q_recv,
    mid_send,
    mid_recv,
    o_send,
    o_recv,
    half_recv,
    x_send,
    x_recv,
):
    z = lax.axis_index("seq")
    x = lax.axis_index("head")
    c = lax.axis_index("tile")
    rows = q_hbm.shape[0]
    columns = w_hbm.shape[1]
    pairs = own.shape[0]
    heads_here = 2 * pairs
    half = z // 2
    inner_z, outer_z = 1 + half, 3 * half
    inner = z == inner_z
    outer = z == outer_z
    send_order = [2, 3, 0, 1, 4, 5]
    take_order = [0, 1, 4, 2, 5, 3]

    def x_ahead(f):
        return lax.rem(x + f, nx)

    def x_behind(f):
        return lax.rem(x - f + nx, nx)

    def head_of(j, t):
        if j < 2:
            return 4 * half + 2 * j + t
        if j < 4:
            return 4 * (1 - half) + 2 * (j - 2) + t
        return 2 * j + t

    def place(j):
        return j + 2 if j < 4 else j - 4

    def block(b):
        return pl.ds(pl.multiple_of(b * rows, rows), rows)

    def columns_of(j, t):
        return pl.ds(pl.multiple_of(head_of(j, t) * HD, HD), HD)

    arguments = (q_hbm, k_hbm, v_hbm)

    def load(j, t):
        for a in range(3):
            pltpu.make_async_copy(
                arguments[a].at[:, columns_of(j, t)], own.at[j, t, a], load_sem.at[j, t]
            ).start()

    def loaded(j, t):
        pltpu.make_async_copy(own.at[j, t], own.at[j, t], load_sem.at[j, t]).wait()

    def big_load(j):
        for a in range(3):
            pltpu.make_async_copy(
                arguments[a].at[:, columns_of(j, c)],
                big.at[place(j), a, block(3)],
                big_sem.at[place(j)],
            ).start()

    for j in send_order:
        for t in range(2):
            load(j, t)

    barrier = pltpu.get_barrier_semaphore()
    pl.semaphore_signal(barrier, inc=1, device_id={"tile": 1 - c}, device_id_type=MESH)
    for f in range(1, nx):
        pl.semaphore_signal(barrier, inc=1, device_id={"head": x_ahead(f)}, device_id_type=MESH)

    @pl.when(inner)
    def _():
        pl.semaphore_signal(barrier, inc=1, device_id={"seq": 3 - z}, device_id_type=MESH)
        pl.semaphore_wait(barrier, nx + 1)
        for t in range(2):
            pl.semaphore_signal(
                barrier, inc=1, device_id={"seq": outer_z, "tile": t}, device_id_type=MESH
            )

    @pl.when(outer)
    def _():
        pl.semaphore_wait(barrier, nx + 2)

    def in_copy(j, t, b, device, span, send_sem):
        low, high = span
        at = place(j)
        if j < 2:
            recv_sem = home_recv.at[j]
        elif high == 1:
            recv_sem = q_recv.at[at]
        else:
            recv_sem = in_recv.at[j - 2, b]
        dst = rel.at[j - 2, :, block(b)] if j in (2, 3) else big.at[at, low:high, block(b)]
        return pltpu.make_async_remote_copy(
            src_ref=own.at[j, t, low:high],
            dst_ref=dst,
            send_sem=send_sem,
            recv_sem=recv_sem,
            device_id=device,
            device_id_type=MESH,
        )

    def sibling_copy(j):
        return in_copy(j, 1 - c, 2, {"tile": 1 - c}, (0, 3), sib_send)

    def landed(ref, send_sem, recv_sem):
        return pltpu.make_async_remote_copy(
            src_ref=ref,
            dst_ref=ref,
            send_sem=send_sem,
            recv_sem=recv_sem,
            device_id={"tile": 1 - c},
            device_id_type=MESH,
        )

    def mid_copy(j, b, send_sem):
        if j < 4:
            at, low = j, 0
            src = own.at[j, c] if b == 3 else rel.at[j - 2, :, block(b)]
        else:
            at, low = place(j), 1
            src = own.at[j, c, 1:3] if b == 3 else big.at[at, 1:3, block(b)]
        return pltpu.make_async_remote_copy(
            src_ref=src,
            dst_ref=big.at[at, low:3, block(4 + b)],
            send_sem=send_sem,
            recv_sem=mid_recv.at[at],
            device_id={"seq": 3 - z},
            device_id_type=MESH,
        )

    def feature(j, t, f):
        if j in LAST:
            start = (2 * nx * LAST.index(j) + 2 * f + t) * HD
            return rows_out.at[:, pl.ds(pl.multiple_of(start, HD), HD)]
        return att.at[j, f, t]

    def peers(j):
        if j in LAST:
            start = 2 * nx * LAST.index(j) * HD
            return rows_out.at[:, start + 2 * HD : start + 2 * nx * HD]
        return att.at[j, 1:nx]

    def weights_of(j):
        if j in LAST:
            start = 2 * nx * LAST.index(j) * HD
            return w_out.at[start : start + 2 * nx * HD]
        return w_buf.at[j]

    def o_copy(j, b, far=0, send_sem=None):
        there = half + far * (1 - 2 * half)
        is_inner = b // 2
        flip = ((b + 1) // 2) % 2
        return pltpu.make_async_remote_copy(
            src_ref=o_out.at[place(j), 4 * far + b],
            dst_ref=feature(j + 2 * far, c, 0),
            send_sem=o_send.at[place(j)] if send_sem is None else send_sem,
            recv_sem=o_recv.at[j + 2 * far, c],
            device_id={
                "seq": is_inner * (1 + there) + (1 - is_inner) * 3 * there,
                "tile": (c + flip) % 2,
            },
            device_id_type=MESH,
        )

    def half_rows(h):
        return pl.ds(h * (rows // 2), rows // 2)

    def o_half_copy(h, send_sem):
        return pltpu.make_async_remote_copy(
            src_ref=o_out.at[place(1), 6, half_rows(h)],
            dst_ref=feature(3, c, 0).at[half_rows(h)],
            send_sem=send_sem,
            recv_sem=half_recv if h else o_recv.at[3, c],
            device_id={"seq": 3 - z, "tile": 1 - c},
            device_id_type=MESH,
        )

    def o_arrival(j, t):
        return pltpu.make_async_remote_copy(
            src_ref=o_out.at[0, 0],
            dst_ref=feature(j, t, 0),
            send_sem=o_send.at[0],
            recv_sem=o_recv.at[j, t],
            device_id={"tile": 1 - c},
            device_id_type=MESH,
        )

    def own_copy(j):
        return pltpu.make_async_copy(o_out.at[place(j), 3], feature(j, c, 0), own_sem)

    def x_copy(j, t, f, src=None):
        return pltpu.make_async_remote_copy(
            src_ref=feature(j, t, 0) if src is None else src,
            dst_ref=feature(j, t, f),
            send_sem=x_send.at[j],
            recv_sem=x_recv.at[j],
            device_id={"head": x_ahead(f)},
            device_id_type=MESH,
        )

    queue = [(j, b, 0) for j in (2, 3) for b in (3, 2)]
    queue += [(j, b, 0) for j in (2, 3) for b in (0, 1)]
    queue += [(j, b, 0) for j in (4, 5) for b in (3, 2)]
    queue += [(j, b, 0) for j in (4, 5) for b in (0, 1)]
    queue += [(0, 0, 1), (0, 3, 1), (0, 1, 1), (1, 0, 1)]
    queue += [(0, 2, 1), (1, 1, 1), (1, 3, 1), (1, 2, 2), (1, 2, 3)]

    def queued(n):
        j, b, far = queue[n]
        send_sem = mid_send.at[n % WINDOW]
        if far > 1:
            return o_half_copy(far - 2, send_sem)
        return o_copy(j, b, 1, send_sem) if far else mid_copy(j, b, send_sem)

    def pump(first, end=None):
        for n in range(first, first + 1 if end is None else end):
            j, b, far = queue[n]
            if not far:
                if b == 3:
                    loaded(j, c)
                else:
                    span = (1, 3) if j > 3 and b < 2 else (0, 3)
                    in_copy(j, c, b, {"tile": 1 - c}, span, sib_send).wait_recv()
            if n >= WINDOW:
                queued(n - WINDOW).wait_send()
            queued(n).start()

    def pumps(*steps):
        return [(at, functools.partial(pump, n)) for at, n in steps]

    def send_sibling(j):
        loaded(j, 1 - c)
        sibling_copy(j).start()

    @pl.when(inner)
    def _():
        pump(0)
        send_sibling(2)
        send_sibling(3)
        pump(1)
        for j in (0, 1, 4, 5):
            send_sibling(j)
        for j in (0, 1):
            loaded(j, c)
        for j in (0, 1, 4, 5):
            big_load(j)

    for j in take_order:
        weights = weights_of(j)
        for t in range(2):
            for f in range(nx):
                head = x_behind(f) * heads_here + head_of(j, t)
                pltpu.make_async_copy(
                    w_hbm.at[pl.ds(pl.multiple_of(head * HD, HD), HD)],
                    weights.at[pl.ds((2 * f + t) * HD, HD)],
                    w_sem.at[j],
                ).start()

    def weights_loaded(j):
        weights = weights_of(j)
        pltpu.make_async_copy(weights, weights, w_sem.at[j]).wait()

    factor = math.log2(math.e) / math.sqrt(HD)
    keys = 8 * rows
    early = 4 * rows // PART * PART

    def fold(at, b, low, high, state=None):
        queries = big[at, 0, block(b)]
        for start in range(low, high, PART):
            span = pl.ds(start, PART)
            scores = lax.dot_general(
                queries,
                big[at, 1, span],
                (((1,), (1,)), ((), ())),
                preferred_element_type=jnp.float32,
            )
            new_max = jnp.max(scores, axis=1, keepdims=True)
            if state is not None:
                row_max, denominator, numerator = state
                new_max = jnp.maximum(row_max, new_max)
            weights = jnp.exp2((scores - new_max) * factor)
            total = jnp.sum(weights, axis=1, keepdims=True)
            product = jnp.dot(
                weights.astype(jnp.bfloat16), big[at, 2, span], preferred_element_type=jnp.float32
            )
            if state is not None:
                scale = jnp.exp2((row_max - new_max) * factor)
                total = denominator * scale + total
                product = numerator * scale + product
            state = new_max, total, product
        return state

    def ready(j):
        at = place(j)
        pltpu.make_async_copy(own.at[j, c], own.at[j, c], big_sem.at[at]).wait()
        if j < 2:
            landed(big.at[at, :, : 3 * rows], sib_send, home_recv.at[j]).wait_recv()
        else:
            landed(big.at[at, 0, : 2 * rows], sib_send, q_recv.at[at]).wait_recv()

    def ready_far(j):
        at = place(j)
        low = 0 if j < 2 else 1
        landed(big.at[at, low:3, 4 * rows :], sib_send, mid_recv.at[at]).wait_recv()

    def begin(j):
        at = place(j)

        def step(b, carry):
            row_max, denominator, num_buf[at, b] = fold(at, b, 0, early)
            max_buf[at, b] = jnp.broadcast_to(row_max, (rows, HD))
            sum_buf[at, b] = jnp.broadcast_to(denominator, (rows, HD))
            return carry

        lax.fori_loop(0, 4, step, 0)

    def compute(j, between):
        at = place(j)
        count = 8 if j < 2 else 4

        def step(i, carry):
            if j < 2:
                b = (i + 4) % 8
                _, denominator, numerator = fold(at, b, 0, keys)
            else:
                b = i
                row_max, denominator, numerator = fold(at, b, early, keys)
                row_max = jnp.broadcast_to(row_max, (rows, HD))
                new_max = jnp.maximum(max_buf[at, b], row_max)
                before = jnp.exp2((max_buf[at, b] - new_max) * factor)
                after = jnp.exp2((row_max - new_max) * factor)
                denominator = sum_buf[at, b] * before + denominator * after
                numerator = num_buf[at, b] * before + numerator * after
            o_out[at, b] = (numerator / denominator).astype(jnp.bfloat16)

            @pl.when(b < 3)
            def _():
                o_copy(j, b).start()

            for when, todo in between:
                pl.when(i == when)(todo)

            return carry

        lax.fori_loop(0, count, step, 0)
        for f in range(1, nx):
            x_copy(j, c, f, o_out.at[at, 3]).start()
        if j in LAST:
            own_copy(j).start()
        else:
            att[j, 0, c] = o_out[at, 3]

    def take(j, t):
        o_arrival(j, t).wait_recv()
        for f in range(1, nx):
            x_copy(j, t, f).start()

    def take_half(h):
        t = 1 - c
        there = feature(3, t, 0).at[half_rows(h)]
        landed(there, sib_send, half_recv if h else o_recv.at[3, t]).wait_recv()
        for f in range(1, nx):
            pltpu.make_async_remote_copy(
                src_ref=there,
                dst_ref=feature(3, t, f).at[half_rows(h)],
                send_sem=x_send.at[3],
                recv_sem=x_recv.at[3],
                device_id={"head": x_ahead(f)},
                device_id_type=MESH,
            ).start()

    def take_outer(j):
        @pl.when(outer)
        def _():
            take(j, c)
            take(j, 1 - c)

    @pl.when(outer)
    def _():
        edges = [(j, t, (0, 3)) for j in (2, 3, 0, 1) for t in range(2)]
        edges += [(j, t, (1, 3)) for j in (4, 5) for t in range(2)]
        edges += [(j, t, (0, 1)) for j in (4, 5) for t in range(2)]

        def edge(n):
            j, t, span = edges[n]
            device = {"seq": inner_z, "tile": t}
            return in_copy(j, t, (c + t) % 2, device, span, edge_send.at[n % WINDOW])

        for n, (j, t, (_, high)) in enumerate(edges):
            if high == 3:
                loaded(j, t)
            if n >= WINDOW:
                edge(n - WINDOW).wait_send()
            edge(n).start()
            if n in (13, 15):
                take(n // 15, c)
                take(n // 15, 1 - c)
        for n in range(len(edges) - WINDOW, len(edges)):
            edge(n).wait_send()

    width = math.gcd(columns, 512)

    def project(j, first=False, last=False):
        weights_loaded(j)
        landed(peers(j), x_send.at[j], x_recv.at[j]).wait_recv()
        rows_in = jnp.concatenate([att[j, f, t] for f in range(nx) for t in range(2)], axis=1)
        for start in range(0, columns, width):
            cols = slice(start, start + width)
            part = jnp.dot(rows_in, w_buf[j, :, cols], preferred_element_type=jnp.float32)
            total = part if first else acc[:, cols] + part
            acc[:, cols] = total
            if last:
                pltpu.make_async_copy(acc.at[:, cols], acc_out.at[:, cols], out_sem).start()

    @pl.when(inner)
    def _():
        pump(2, 9)
        ready(0)
        ready_far(0)
        compute(0, pumps((3, 9), (6, 10)))
        ready(1)
        ready_far(1)
        compute(1, pumps((1, 11), (4, 12), (7, 13)) + [(0, functools.partial(take, 0, 1 - c))])
        take(1, 1 - c)
        pump(14)

    project(0, first=True)

    @pl.when(inner)
    def _():
        ready(4)
        begin(4)
        pump(15)

    project(1)

    @pl.when(inner)
    def _():
        ready_far(4)
        compute(4, pumps((2, 16)))
        ready(5)
        begin(5)
        pump(17)
        pump(18)
        ready_far(5)
        taken = [(0, functools.partial(take, 4, 1 - c)), (2, functools.partial(take, 2, c))]
        compute(5, pumps((1, 19), (3, 20)) + taken)
        take(5, 1 - c)
        pump(21)

    take_outer(4)
    take_outer(2)
    project(4)

    @pl.when(outer)
    def _():
        take(5, c)
        take(3, c)
        take(5, 1 - c)
        take(3, 1 - c)

    @pl.when(inner)
    def _():
        pump(22, 24)
        take(2, 1 - c)
        pump(24)
        take(3, c)
        take_half(0)
        take_half(1)

    project(2, last=True)
    pltpu.make_async_copy(acc, acc_out, out_sem).wait()
    for j in LAST:
        weights_loaded(j)
    for j in LAST:
        landed(peers(j), x_send.at[j], x_recv.at[j]).wait_recv()

    @pl.when(inner)
    def _():
        own_copy(5).wait()

    @pl.when(inner)
    def _():
        landed(own.at[:, 0], sib_send, sib_send).wait_send()
        for at in range(o_out.shape[0]):
            landed(o_out.at[at, :3], o_send.at[at], sib_send).wait_send()
        for n in range(len(queue) - WINDOW, len(queue)):
            queued(n).wait_send()

    for j in range(pairs):
        landed(att.at[j, 1:nx], x_send.at[j], sib_send).wait_send()


def exchanged(nx, query_states, key_states, value_states, out_weight, residual, gate_scale):
    rows, width = query_states.shape
    columns = out_weight.shape[1]
    pairs = width // HD // 2
    jobs = pairs - 2
    bf16 = jnp.bfloat16
    dma = pltpu.SemaphoreType.DMA
    anywhere = pl.BlockSpec(memory_space=pltpu.HBM)
    acc, rows_in, last_weight = pl.pallas_call(
        functools.partial(kernel, nx),
        out_shape=[
            jax.ShapeDtypeStruct((rows, columns), jnp.float32),
            jax.ShapeDtypeStruct((rows, 2 * len(LAST) * nx * HD), bf16),
            jax.ShapeDtypeStruct((2 * len(LAST) * nx * HD, columns), bf16),
        ],
        in_specs=[anywhere] * 4,
        out_specs=[pl.BlockSpec(memory_space=pl.ANY)] * 3,
        scratch_shapes=[
            pltpu.VMEM((pairs, 2, 3, rows, HD), bf16),
            pltpu.VMEM((jobs, 3, 8 * rows, HD), bf16),
            pltpu.VMEM((2, 3, 3 * rows, HD), bf16),
            pltpu.VMEM((jobs, 8, rows, HD), bf16),
            pltpu.VMEM((pairs, nx, 2, rows, HD), bf16),
            pltpu.VMEM((pairs, 2 * nx * HD, columns), bf16),
            pltpu.VMEM((rows, columns), jnp.float32),
            pltpu.VMEM((2, 4, rows, HD), jnp.float32),
            pltpu.VMEM((2, 4, rows, HD), jnp.float32),
            pltpu.VMEM((2, 4, rows, HD), jnp.float32),
            dma,
            dma,
            dma((pairs, 2)),
            dma((jobs,)),
            dma((pairs,)),
            dma((WINDOW,)),
            dma,
            dma((pairs - 2, 3)),
            dma((2,)),
            dma((2,)),
            dma((WINDOW,)),
            dma((jobs,)),
            dma((jobs,)),
            dma((pairs, 2)),
            dma,
            dma((pairs,)),
            dma((pairs,)),
        ],
        compiler_params=pltpu.CompilerParams(
            collective_id=0, has_side_effects=True, vmem_limit_bytes=44 << 20
        ),
    )(
        *(
            pltpu.with_memory_space_constraint(array, pltpu.HBM)
            for array in (query_states, key_states, value_states, out_weight)
        )
    )
    projected = acc + jnp.dot(rows_in, last_weight, preferred_element_type=jnp.float32)
    return (residual.astype(jnp.float32) + gate_scale[None, :] * projected).astype(bf16)


def solution(mesh):
    n, nx = mesh.shape["seq"], mesh.shape["head"]

    def per_device(query_states, key_states, value_states, residual, out_weight, gate_scale):
        heads_here = query_states.shape[1] // HD
        fits = query_states.shape[0] % 32 == 0 and 8 * query_states.shape[0] % PART == 0
        if n != 4 or nx < 2 or mesh.shape["tile"] != 2 or heads_here != 12 or not fits:
            return gathered(
                query_states, key_states, value_states, residual, out_weight, gate_scale
            )
        return exchanged(
            nx, query_states, key_states, value_states, out_weight, residual, gate_scale
        )

    placed = (
        P(("groups", "seq", "tile"), "head"),
        P(("groups", "seq", "tile"), "head"),
        P(("groups", "seq", "tile"), "head"),
        P(("groups", "seq", "tile"), "head"),
        P(None, "head"),
        P(("groups", "head")),
    )
    return jax.shard_map(
        per_device,
        mesh=mesh,
        in_specs=placed,
        out_specs=P(("groups", "seq", "tile"), "head"),
        check_vma=False,
    )
```

```python
import functools
import math

import jax
import jax.numpy as jnp
from jax import lax
from jax.experimental import pallas as pl
from jax.experimental.pallas import tpu as pltpu
from jax.sharding import PartitionSpec as P

HD = 128
MESH = pl.DeviceIdType.MESH


def gathered(query_states, key_states, value_states, residual, out_weight, gate_scale):
    row_count = query_states.shape[0]
    heads_here = query_states.shape[1] // HD
    score_scale = 1.0 / math.sqrt(HD)
    query_heads = query_states.reshape(row_count, heads_here, HD)
    key_heads = lax.all_gather(key_states, ("seq", "tile"), axis=0, tiled=True).reshape(
        -1, heads_here, HD
    )
    value_heads = lax.all_gather(value_states, ("seq", "tile"), axis=0, tiled=True).reshape(
        -1, heads_here, HD
    )
    scores = (
        jnp.einsum("qhd,khd->hqk", query_heads, key_heads, preferred_element_type=jnp.float32)
        * score_scale
    )
    row_max = jnp.max(scores, axis=2)
    weights = jnp.exp(scores - row_max[:, :, None])
    denominator = jnp.sum(weights, axis=2)
    numerator = jnp.einsum(
        "hqk,khd->qhd",
        weights.astype(jnp.bfloat16),
        value_heads,
        preferred_element_type=jnp.float32,
    )
    attended = (
        (numerator / denominator.T[:, :, None])
        .astype(jnp.bfloat16)
        .reshape(row_count, heads_here * HD)
    )
    projected = jnp.dot(
        lax.all_gather(attended, "head", axis=1, tiled=True),
        out_weight,
        preferred_element_type=jnp.float32,
    )
    return (residual.astype(jnp.float32) + gate_scale[None, :] * projected).astype(jnp.bfloat16)


WINDOW = 3
EDGE = 2
LAST = (5, 3)
PART = 256


def kernel(
    nx,
    q_hbm,
    k_hbm,
    v_hbm,
    w_hbm,
    acc_out,
    rows_out,
    w_out,
    own,
    big,
    rel,
    o_out,
    att,
    w_buf,
    acc,
    max_buf,
    sum_buf,
    num_buf,
    out_sem,
    own_sem,
    load_sem,
    big_sem,
    w_sem,
    edge_send,
    sib_send,
    in_recv,
    home_recv,
    q_recv,
    mid_send,
    mid_recv,
    o_send,
    o_recv,
    x_send,
    x_recv,
):
    z = lax.axis_index("seq")
    x = lax.axis_index("head")
    c = lax.axis_index("tile")
    rows = q_hbm.shape[0]
    columns = w_hbm.shape[1]
    pairs = own.shape[0]
    heads_here = 2 * pairs
    half = z // 2
    inner_z, outer_z = 1 + half, 3 * half
    inner = z == inner_z
    outer = z == outer_z
    send_order = [2, 3, 0, 1, 4, 5]
    take_order = [0, 1, 4, 2, 5, 3]

    def x_ahead(f):
        return lax.rem(x + f, nx)

    def x_behind(f):
        return lax.rem(x - f + nx, nx)

    def head_of(j, t):
        if j < 2:
            return 4 * half + 2 * j + t
        if j < 4:
            return 4 * (1 - half) + 2 * (j - 2) + t
        return 2 * j + t

    def place(j):
        return j + 2 if j < 4 else j - 4

    def block(b):
        return pl.ds(pl.multiple_of(b * rows, rows), rows)

    def columns_of(j, t):
        return pl.ds(pl.multiple_of(head_of(j, t) * HD, HD), HD)

    arguments = (q_hbm, k_hbm, v_hbm)

    def load(j, t):
        for a in range(3):
            pltpu.make_async_copy(
                arguments[a].at[:, columns_of(j, t)], own.at[j, t, a], load_sem.at[j, t]
            ).start()

    def loaded(j, t):
        pltpu.make_async_copy(own.at[j, t], own.at[j, t], load_sem.at[j, t]).wait()

    def big_load(j):
        for a in range(3):
            pltpu.make_async_copy(
                arguments[a].at[:, columns_of(j, c)],
                big.at[place(j), a, block(3)],
                big_sem.at[place(j)],
            ).start()

    for j in send_order:
        for t in range(2):
            load(j, t)

    barrier = pltpu.get_barrier_semaphore()
    pl.semaphore_signal(barrier, inc=1, device_id={"tile": 1 - c}, device_id_type=MESH)
    for f in range(1, nx):
        pl.semaphore_signal(barrier, inc=1, device_id={"head": x_ahead(f)}, device_id_type=MESH)

    @pl.when(inner)
    def _():
        pl.semaphore_signal(barrier, inc=1, device_id={"seq": 3 - z}, device_id_type=MESH)
        pl.semaphore_wait(barrier, nx + 1)
        for t in range(2):
            pl.semaphore_signal(
                barrier, inc=1, device_id={"seq": outer_z, "tile": t}, device_id_type=MESH
            )

    @pl.when(outer)
    def _():
        pl.semaphore_wait(barrier, nx + 2)

    def in_copy(j, t, b, device, span, send_sem):
        low, high = span
        at = place(j)
        if j < 2:
            recv_sem = home_recv.at[j]
        elif high == 1:
            recv_sem = q_recv.at[at]
        else:
            recv_sem = in_recv.at[j - 2, b]
        dst = rel.at[j - 2, :, block(b)] if j in (2, 3) else big.at[at, low:high, block(b)]
        return pltpu.make_async_remote_copy(
            src_ref=own.at[j, t, low:high],
            dst_ref=dst,
            send_sem=send_sem,
            recv_sem=recv_sem,
            device_id=device,
            device_id_type=MESH,
        )

    def sibling_copy(j):
        return in_copy(j, 1 - c, 2, {"tile": 1 - c}, (0, 3), sib_send)

    def landed(ref, send_sem, recv_sem):
        return pltpu.make_async_remote_copy(
            src_ref=ref,
            dst_ref=ref,
            send_sem=send_sem,
            recv_sem=recv_sem,
            device_id={"tile": 1 - c},
            device_id_type=MESH,
        )

    def mid_copy(j, b, send_sem):
        if j < 4:
            at, low = j, 0
            src = own.at[j, c] if b == 3 else rel.at[j - 2, :, block(b)]
        else:
            at, low = place(j), 1
            src = own.at[j, c, 1:3] if b == 3 else big.at[at, 1:3, block(b)]
        return pltpu.make_async_remote_copy(
            src_ref=src,
            dst_ref=big.at[at, low:3, block(4 + b)],
            send_sem=send_sem,
            recv_sem=mid_recv.at[at],
            device_id={"seq": 3 - z},
            device_id_type=MESH,
        )

    def feature(j, t, f):
        if j in LAST:
            start = (2 * nx * LAST.index(j) + 2 * f + t) * HD
            return rows_out.at[:, pl.ds(pl.multiple_of(start, HD), HD)]
        return att.at[j, f, t]

    def peers(j):
        if j in LAST:
            start = 2 * nx * LAST.index(j) * HD
            return rows_out.at[:, start + 2 * HD : start + 2 * nx * HD]
        return att.at[j, 1:nx]

    def weights_of(j):
        if j in LAST:
            start = 2 * nx * LAST.index(j) * HD
            return w_out.at[start : start + 2 * nx * HD]
        return w_buf.at[j]

    def o_copy(j, b, far=0, send_sem=None):
        there = half + far * (1 - 2 * half)
        is_inner = b // 2
        flip = ((b + 1) // 2) % 2
        return pltpu.make_async_remote_copy(
            src_ref=o_out.at[place(j), 4 * far + b],
            dst_ref=feature(j + 2 * far, c, 0),
            send_sem=o_send.at[place(j)] if send_sem is None else send_sem,
            recv_sem=o_recv.at[j + 2 * far, c],
            device_id={
                "seq": is_inner * (1 + there) + (1 - is_inner) * 3 * there,
                "tile": (c + flip) % 2,
            },
            device_id_type=MESH,
        )

    def o_arrival(j, t):
        return pltpu.make_async_remote_copy(
            src_ref=o_out.at[0, 0],
            dst_ref=feature(j, t, 0),
            send_sem=o_send.at[0],
            recv_sem=o_recv.at[j, t],
            device_id={"tile": 1 - c},
            device_id_type=MESH,
        )

    def own_copy(j):
        return pltpu.make_async_copy(o_out.at[place(j), 3], feature(j, c, 0), own_sem)

    def x_copy(j, t, f, src=None):
        return pltpu.make_async_remote_copy(
            src_ref=feature(j, t, 0) if src is None else src,
            dst_ref=feature(j, t, f),
            send_sem=x_send.at[j],
            recv_sem=x_recv.at[j],
            device_id={"head": x_ahead(f)},
            device_id_type=MESH,
        )

    queue = [(j, b, 0) for j in (2, 3) for b in (3, 2)]
    queue += [(j, b, 0) for j in (2, 3) for b in (0, 1)]
    queue += [(j, b, 0) for j in (4, 5) for b in (3, 2)]
    queue += [(j, b, 0) for j in (4, 5) for b in (0, 1)]
    queue += [(0, 0, 1), (0, 3, 1), (0, 1, 1), (1, 0, 1)]
    queue += [(0, 2, 1), (1, 1, 1), (1, 3, 1), (1, 2, 1)]

    def queued(n):
        j, b, far = queue[n]
        send_sem = mid_send.at[n % WINDOW]
        return o_copy(j, b, 1, send_sem) if far else mid_copy(j, b, send_sem)

    def pump(first, end=None):
        for n in range(first, first + 1 if end is None else end):
            j, b, far = queue[n]
            if not far:
                if b == 3:
                    loaded(j, c)
                else:
                    span = (1, 3) if j > 3 and b < 2 else (0, 3)
                    in_copy(j, c, b, {"tile": 1 - c}, span, sib_send).wait_recv()
            if n >= WINDOW:
                queued(n - WINDOW).wait_send()
            queued(n).start()

    def pumps(*steps):
        return [(at, functools.partial(pump, n)) for at, n in steps]

    def send_sibling(j):
        loaded(j, 1 - c)
        sibling_copy(j).start()

    @pl.when(inner)
    def _():
        pump(0)
        send_sibling(2)
        send_sibling(3)
        pump(1)
        for j in (0, 1, 4, 5):
            send_sibling(j)
        for j in (0, 1):
            loaded(j, c)
        for j in (0, 1, 4, 5):
            big_load(j)

    for j in take_order:
        weights = weights_of(j)
        for t in range(2):
            for f in range(nx):
                head = x_behind(f) * heads_here + head_of(j, t)
                pltpu.make_async_copy(
                    w_hbm.at[pl.ds(pl.multiple_of(head * HD, HD), HD)],
                    weights.at[pl.ds((2 * f + t) * HD, HD)],
                    w_sem.at[j],
                ).start()

    def weights_loaded(j):
        weights = weights_of(j)
        pltpu.make_async_copy(weights, weights, w_sem.at[j]).wait()

    factor = math.log2(math.e) / math.sqrt(HD)
    keys = 8 * rows
    early = 4 * rows // PART * PART

    def fold(at, b, low, high, state=None):
        queries = big[at, 0, block(b)]
        for start in range(low, high, PART):
            span = pl.ds(start, PART)
            scores = lax.dot_general(
                queries,
                big[at, 1, span],
                (((1,), (1,)), ((), ())),
                preferred_element_type=jnp.float32,
            )
            new_max = jnp.max(scores, axis=1, keepdims=True)
            if state is not None:
                row_max, denominator, numerator = state
                new_max = jnp.maximum(row_max, new_max)
            weights = jnp.exp2((scores - new_max) * factor)
            total = jnp.sum(weights, axis=1, keepdims=True)
            product = jnp.dot(
                weights.astype(jnp.bfloat16), big[at, 2, span], preferred_element_type=jnp.float32
            )
            if state is not None:
                scale = jnp.exp2((row_max - new_max) * factor)
                total = denominator * scale + total
                product = numerator * scale + product
            state = new_max, total, product
        return state

    def ready(j):
        at = place(j)
        pltpu.make_async_copy(own.at[j, c], own.at[j, c], big_sem.at[at]).wait()
        if j < 2:
            landed(big.at[at, :, : 3 * rows], sib_send, home_recv.at[j]).wait_recv()
        else:
            landed(big.at[at, 0, : 2 * rows], sib_send, q_recv.at[at]).wait_recv()

    def ready_far(j):
        at = place(j)
        low = 0 if j < 2 else 1
        landed(big.at[at, low:3, 4 * rows :], sib_send, mid_recv.at[at]).wait_recv()

    def begin(j):
        at = place(j)

        def step(b, carry):
            row_max, denominator, num_buf[at, b] = fold(at, b, 0, early)
            max_buf[at, b] = jnp.broadcast_to(row_max, (rows, HD))
            sum_buf[at, b] = jnp.broadcast_to(denominator, (rows, HD))
            return carry

        lax.fori_loop(0, 4, step, 0)

    def compute(j, between):
        at = place(j)
        count = 8 if j < 2 else 4

        def step(i, carry):
            if j < 2:
                b = (i + 4) % 8
                _, denominator, numerator = fold(at, b, 0, keys)
            else:
                b = i
                row_max, denominator, numerator = fold(at, b, early, keys)
                row_max = jnp.broadcast_to(row_max, (rows, HD))
                new_max = jnp.maximum(max_buf[at, b], row_max)
                before = jnp.exp2((max_buf[at, b] - new_max) * factor)
                after = jnp.exp2((row_max - new_max) * factor)
                denominator = sum_buf[at, b] * before + denominator * after
                numerator = num_buf[at, b] * before + numerator * after
            o_out[at, b] = (numerator / denominator).astype(jnp.bfloat16)

            @pl.when(b < 3)
            def _():
                o_copy(j, b).start()

            for when, todo in between:
                pl.when(i == when)(todo)

            return carry

        lax.fori_loop(0, count, step, 0)
        for f in range(1, nx):
            x_copy(j, c, f, o_out.at[at, 3]).start()
        if j in LAST:
            own_copy(j).start()
        else:
            att[j, 0, c] = o_out[at, 3]

    def take(j, t):
        o_arrival(j, t).wait_recv()
        for f in range(1, nx):
            x_copy(j, t, f).start()

    def take_outer(j):
        @pl.when(outer)
        def _():
            take(j, c)
            take(j, 1 - c)

    @pl.when(outer)
    def _():
        edges = [(j, t, (0, 3)) for j in (2, 3, 0, 1) for t in range(2)]
        edges += [(j, t, (1, 3)) for j in (4, 5) for t in range(2)]
        edges += [(j, t, (0, 1)) for j in (4, 5) for t in range(2)]

        def edge(n):
            j, t, span = edges[n]
            device = {"seq": inner_z, "tile": t}
            return in_copy(j, t, (c + t) % 2, device, span, edge_send.at[n % EDGE])

        for n, (j, t, (_, high)) in enumerate(edges):
            if high == 3:
                loaded(j, t)
            if n >= EDGE:
                edge(n - EDGE).wait_send()
            edge(n).start()
            if n in (13, 15):
                take(n // 15, c)
                take(n // 15, 1 - c)
        for n in range(len(edges) - EDGE, len(edges)):
            edge(n).wait_send()

    width = math.gcd(columns, 512)

    def project(j, first=False, last=False):
        weights_loaded(j)
        landed(peers(j), x_send.at[j], x_recv.at[j]).wait_recv()
        rows_in = jnp.concatenate([att[j, f, t] for f in range(nx) for t in range(2)], axis=1)
        for start in range(0, columns, width):
            cols = slice(start, start + width)
            part = jnp.dot(rows_in, w_buf[j, :, cols], preferred_element_type=jnp.float32)
            total = part if first else acc[:, cols] + part
            acc[:, cols] = total
            if last:
                pltpu.make_async_copy(acc.at[:, cols], acc_out.at[:, cols], out_sem).start()

    @pl.when(inner)
    def _():
        pump(2, 9)
        ready(0)
        ready_far(0)
        compute(0, pumps((3, 9), (6, 10)))
        ready(1)
        ready_far(1)
        compute(1, pumps((1, 11), (4, 12), (7, 13)) + [(0, functools.partial(take, 0, 1 - c))])
        take(1, 1 - c)
        pump(14)

    project(0, first=True)

    @pl.when(inner)
    def _():
        ready(4)
        begin(4)
        pump(15)

    project(1)

    @pl.when(inner)
    def _():
        ready_far(4)
        compute(4, pumps((2, 16)))
        ready(5)
        begin(5)
        pump(17)
        pump(18)
        ready_far(5)
        taken = [(0, functools.partial(take, 4, 1 - c))]
        compute(5, pumps((1, 19), (3, 20)) + taken)
        take(5, 1 - c)
        take(2, c)
        pump(21)

    take_outer(4)
    take_outer(2)
    project(4)

    @pl.when(outer)
    def _():
        take(5, c)
        take(3, c)
        take(5, 1 - c)
        take(3, 1 - c)

    @pl.when(inner)
    def _():
        pump(22, 24)
        take(2, 1 - c)
        take(3, c)
        take(3, 1 - c)

    project(2, last=True)
    pltpu.make_async_copy(acc, acc_out, out_sem).wait()
    for j in LAST:
        weights_loaded(j)
    for j in LAST:
        landed(peers(j), x_send.at[j], x_recv.at[j]).wait_recv()

    @pl.when(inner)
    def _():
        own_copy(5).wait()

    @pl.when(inner)
    def _():
        landed(own.at[:, 0], sib_send, sib_send).wait_send()
        for at in range(o_out.shape[0]):
            landed(o_out.at[at, :3], o_send.at[at], sib_send).wait_send()
        for n in range(len(queue) - WINDOW, len(queue)):
            queued(n).wait_send()

    for j in range(pairs):
        landed(att.at[j, 1:nx], x_send.at[j], sib_send).wait_send()


def exchanged(nx, query_states, key_states, value_states, out_weight, residual, gate_scale):
    rows, width = query_states.shape
    columns = out_weight.shape[1]
    pairs = width // HD // 2
    jobs = pairs - 2
    bf16 = jnp.bfloat16
    dma = pltpu.SemaphoreType.DMA
    anywhere = pl.BlockSpec(memory_space=pltpu.HBM)
    acc, rows_in, last_weight = pl.pallas_call(
        functools.partial(kernel, nx),
        out_shape=[
            jax.ShapeDtypeStruct((rows, columns), jnp.float32),
            jax.ShapeDtypeStruct((rows, 2 * len(LAST) * nx * HD), bf16),
            jax.ShapeDtypeStruct((2 * len(LAST) * nx * HD, columns), bf16),
        ],
        in_specs=[anywhere] * 4,
        out_specs=[pl.BlockSpec(memory_space=pl.ANY)] * 3,
        scratch_shapes=[
            pltpu.VMEM((pairs, 2, 3, rows, HD), bf16),
            pltpu.VMEM((jobs, 3, 8 * rows, HD), bf16),
            pltpu.VMEM((2, 3, 3 * rows, HD), bf16),
            pltpu.VMEM((jobs, 8, rows, HD), bf16),
            pltpu.VMEM((pairs, nx, 2, rows, HD), bf16),
            pltpu.VMEM((pairs, 2 * nx * HD, columns), bf16),
            pltpu.VMEM((rows, columns), jnp.float32),
            pltpu.VMEM((2, 4, rows, HD), jnp.float32),
            pltpu.VMEM((2, 4, rows, HD), jnp.float32),
            pltpu.VMEM((2, 4, rows, HD), jnp.float32),
            dma,
            dma,
            dma((pairs, 2)),
            dma((jobs,)),
            dma((pairs,)),
            dma((EDGE,)),
            dma,
            dma((pairs - 2, 3)),
            dma((2,)),
            dma((2,)),
            dma((WINDOW,)),
            dma((jobs,)),
            dma((jobs,)),
            dma((pairs, 2)),
            dma((pairs,)),
            dma((pairs,)),
        ],
        compiler_params=pltpu.CompilerParams(
            collective_id=0, has_side_effects=True, vmem_limit_bytes=44 << 20
        ),
    )(
        *(
            pltpu.with_memory_space_constraint(array, pltpu.HBM)
            for array in (query_states, key_states, value_states, out_weight)
        )
    )
    projected = acc + jnp.dot(rows_in, last_weight, preferred_element_type=jnp.float32)
    return (residual.astype(jnp.float32) + gate_scale[None, :] * projected).astype(bf16)


def solution(mesh):
    n, nx = mesh.shape["seq"], mesh.shape["head"]

    def per_device(query_states, key_states, value_states, residual, out_weight, gate_scale):
        heads_here = query_states.shape[1] // HD
        fits = query_states.shape[0] % 32 == 0 and 8 * query_states.shape[0] % PART == 0
        if n != 4 or nx < 2 or mesh.shape["tile"] != 2 or heads_here != 12 or not fits:
            return gathered(
                query_states, key_states, value_states, residual, out_weight, gate_scale
            )
        return exchanged(
            nx, query_states, key_states, value_states, out_weight, residual, gate_scale
        )

    placed = (
        P(("groups", "seq", "tile"), "head"),
        P(("groups", "seq", "tile"), "head"),
        P(("groups", "seq", "tile"), "head"),
        P(("groups", "seq", "tile"), "head"),
        P(None, "head"),
        P(("groups", "head")),
    )
    return jax.shard_map(
        per_device,
        mesh=mesh,
        in_specs=placed,
        out_specs=P(("groups", "seq", "tile"), "head"),
        check_vma=False,
    )
```
